32 devices in a mesh: groups: 2 (over y), inner: 8 (over z, x), outer: 2 (over core).
Axes of the slice: x: 2, y: 2, z: 4, core: 2. Of those that a mesh axis runs over, the one named last changes fastest.
Arguments:
- queries: bfloat16 [4096, 1024], P(('groups', 'outer', 'inner')), parts along dimension 0, may hold values from -6 to 6
- keys: bfloat16 [4096, 2, 1024], P(('groups', 'outer', 'inner')), parts along dimension 0, may hold values from -6 to 6
- values: bfloat16 [4096, 2, 1024], P(('groups', 'outer', 'inner')), parts along dimension 0, may hold values from -6 to 6
- log_gate: float32 [4096, 8], P(('groups', 'outer', 'inner')), parts along dimension 0, may hold values from -1 to 0, as said below
- out_gate: bfloat16 [4096, 1024], P(('groups', 'outer', 'inner')), parts along dimension 0, may hold values from -6 to 6
- norm_gain: float32 [128], replicated, may hold values from 0.1 to 1.9
Outputs:
- gated_output: bfloat16 [4096, 1024], P(('groups', 'outer', 'inner')), parts along dimension 0
The draws below stay inside these ranges and needn't reach their ends.
There are 2 independent parts, one for each index of `groups`. The reference program is written for one: setup_inputs(seed, part) draws one part's arguments, and reference() takes and returns one part's arrays. A program takes and returns all parts, laid end to end along the dimension named above; an argument that names none is the same for every part. Nothing has to cross between parts.
Inputs may be any that keep to these rules, and one draw needn't show every extreme that they name: `log_gate`: logarithm of the factor by which a head's state is scaled at a token; never positive.
All inputs are finite; a program needn't handle non-finite values.
Results may differ from the reference program's by a relative error of at most 0.001.
Values sent between devices are 32-bit elements; how exact they have to be, the bound alone decides.
A program may use at most 512 MiB of HBM per device.

```python
import jax
import jax.numpy as jnp
from jax import lax

HEAD_GROUP = 8
HEAD = 128
T_DEV = 128
TOKEN_TOTAL = 2048
WIDTH = 1024


def draw_log_gate(key, part):
    complete_keys = jax.random.split(key, 7)
    head_order = jax.random.permutation(complete_keys[0], HEAD_GROUP)
    slow_heads = head_order >= HEAD_GROUP // 2
    fast_rate = jnp.exp(jax.random.uniform(complete_keys[1], (HEAD_GROUP,), jnp.float32, jnp.log(1.0 / 50.0), jnp.log(1.0 / 30.0)))
    slow_rate = jnp.exp(jax.random.uniform(complete_keys[2], (HEAD_GROUP,), jnp.float32, jnp.log(0.05), jnp.log(0.25))) / TOKEN_TOTAL
    baseline_speed = jnp.where(slow_heads, slow_rate, fast_rate)
    random_wobble = jnp.exp(jax.random.uniform(complete_keys[3], (TOKEN_TOTAL, HEAD_GROUP), jnp.float32, jnp.log(0.5), jnp.log(2.0)))
    processor_multiplier = jnp.exp(jax.random.uniform(complete_keys[4], (TOKEN_TOTAL // T_DEV, HEAD_GROUP), jnp.float32, jnp.log(0.5), jnp.log(2.0)))
    processor_multiplier = jnp.repeat(processor_multiplier, T_DEV, axis=0)
    spike_positions = jax.random.randint(complete_keys[5], (2, HEAD_GROUP), 0, TOKEN_TOTAL)
    position_list = jnp.arange(TOKEN_TOTAL)[:, None]
    spike_mask = (position_list == spike_positions[0][None, :]) | (position_list == spike_positions[1][None, :])
    spike_slowdown = jnp.log(jax.random.uniform(complete_keys[6], (TOKEN_TOTAL, HEAD_GROUP), jnp.float32, 0.45, 0.8))
    return jnp.where(spike_mask, spike_slowdown, 0.0) - baseline_speed[None, :] * random_wobble * processor_multiplier


def level_of(stream_key, shape, cuts, smallest, top_value):
    level, own = 1.0, jax.random.fold_in(stream_key, 6)
    for position, shards_of in cuts:
        draws = jnp.exp(jax.random.uniform(jax.random.fold_in(own, position), (shards_of,), jnp.float32, smallest / len(cuts), top_value / len(cuts)))
        level = level * jnp.repeat(draws, shape[position] // shards_of).reshape([-1 if axis == position else 1 for axis in range(len(shape))])
    return level


def centred(rng, extent, spread, limit, shards=(), held_as=jnp.bfloat16):
    level = level_of(rng, extent, shards, -0.22, 0.18) if shards else 1.0
    values = jax.random.normal(rng, extent, jnp.float32) * spread * level
    return jnp.minimum(jnp.maximum(values, -limit), limit).astype(held_as)


def setup_inputs(seed: int = 0, part: int = 0) -> dict:
    splits = jax.random.split(jax.random.key(seed), 7)
    part_keys = jax.random.split(jax.random.fold_in(splits[6], part), 7)
    return {
        "queries": centred(part_keys[0], (TOKEN_TOTAL, WIDTH), 1.0, 6.0, ((0, 16),)),
        "keys": centred(part_keys[1], (TOKEN_TOTAL, 2, WIDTH), 1.0, 6.0, ((0, 16),)),
        "values": centred(part_keys[2], (TOKEN_TOTAL, 2, WIDTH), 1.0, 6.0, ((0, 16),)),
        "log_gate": draw_log_gate(jax.random.fold_in(jax.random.fold_in(splits[6], part), 71), part),
        "out_gate": centred(part_keys[4], (TOKEN_TOTAL, WIDTH), 1.0, 6.0, ((0, 16),)),
        "norm_gain": jnp.clip(1.0 + 0.18 * jax.random.normal(splits[5], (HEAD,), jnp.float32), 0.1, 1.9),
    }


highest = lax.Precision.HIGHEST
eps_norm = 1e-06

def reference(queries, keys, values, log_gate, out_gate, norm_gain):
    tok_count = queries.shape[0]
    query_rows = queries.astype(jnp.float32).reshape(tok_count, HEAD_GROUP, HEAD)
    raw_keys = keys.astype(jnp.float32).reshape(tok_count, 2, HEAD_GROUP, HEAD)
    unit_keys = raw_keys * lax.rsqrt(lax.optimization_barrier(jnp.sum(raw_keys * raw_keys, axis=-1, keepdims=True)) + eps_norm)
    value_rows = values.astype(jnp.float32).reshape(tok_count, 2, HEAD_GROUP, HEAD)
    decay_rows = jnp.exp(log_gate)

    def advance_token(carried_state, inputs):
        query_now, keys_now, values_now, decay_now = inputs
        carried_state = decay_now[:, None, None] * carried_state
        for reflection in range(2):
            unit_key = keys_now[reflection]
            projected = jnp.einsum('hd,hde->he', unit_key, carried_state, precision=highest)
            carried_state = carried_state + 2.0 * unit_key[:, :, None] * (values_now[reflection] - projected)[:, None, :]
        return (carried_state, jnp.einsum('hd,hde->he', query_now, carried_state, precision=highest))
    initial = jnp.zeros((HEAD_GROUP, HEAD, HEAD), jnp.float32)
    final_state, head_outputs = lax.scan(advance_token, initial, (query_rows, unit_keys, value_rows, decay_rows))
    scale_inv = lax.rsqrt(lax.optimization_barrier(jnp.mean(head_outputs * head_outputs, axis=-1, keepdims=True)) + eps_norm)
    gate_vals = jax.nn.silu(out_gate.astype(jnp.float32).reshape(tok_count, HEAD_GROUP, HEAD))
    result = head_outputs * scale_inv * norm_gain * gate_vals
    return result.reshape(tok_count, HEAD_GROUP * HEAD).astype(jnp.bfloat16)
```

```python
import jax
import jax.numpy as jnp
from jax import lax
from jax.experimental import pallas as pl
from jax.experimental.pallas import tpu as pltpu
from jax.sharding import PartitionSpec as P

eps_norm = 1e-06
f32 = jnp.float32
bf16 = jnp.bfloat16
MESH = pl.DeviceIdType.MESH
NT = (((1,), (1,)), ((), ()))
TN = (((0,), (0,)), ((), ()))


def mm(a, b):
    return jnp.dot(a, b, preferred_element_type=f32)


def split2(x):
    hi = x.astype(bf16)
    return hi, (x - hi.astype(f32)).astype(bf16)


def split3(x):
    hi, rest = x.astype(bf16), None
    rest = x - hi.astype(f32)
    mid = rest.astype(bf16)
    return hi, mid, (rest - mid.astype(f32)).astype(bf16)


def wide(x):
    return jnp.concatenate(split2(x), axis=1)


def square(x):
    row = jnp.concatenate(split2(x), axis=1)
    return jnp.concatenate([row, row], axis=0)


def mm4(a_wide, b_square, size):
    both = mm(a_wide, b_square)
    return both[:, :size] + both[:, size:]


def local_kernel(k_ref, v_ref, q_ref, lg_ref, aw_ref, b_ref, r_ref, lo_ref):
    steps = k_ref.shape[0]
    toks = q_ref.shape[0]
    heads = lg_ref.shape[0]
    d = k_ref.shape[1] // heads
    half = steps // 2

    def iotas(r, c):
        return (
            lax.broadcasted_iota(jnp.int32, (r, c), 0),
            lax.broadcasted_iota(jnp.int32, (r, c), 1),
        )

    i_st, j_tk = iotas(steps, toks)
    tri_steps = (j_tk <= i_st // 2).astype(f32).astype(bf16)
    i_tk, j_tk2 = iotas(toks, toks)
    tri_toks = (j_tk2 <= i_tk).astype(f32).astype(bf16)
    lgs = split3(lg_ref[...])

    def nt(a, b):
        return lax.dot_general(a, b, NT, preferred_element_type=f32)

    c_col = sum(nt(tri_steps, p) for p in lgs)
    q_col = sum(nt(tri_toks, p) for p in lgs)
    c_row = sum(nt(p, tri_steps) for p in lgs)
    ii, jj = iotas(steps, steps)
    strict = ii > jj
    it, jt = iotas(toks, steps)
    visible = jt <= 2 * it + 1
    hi_, hj_ = iotas(half, half)
    eye = (hi_ == hj_).astype(f32)
    eye_d = (lax.broadcasted_iota(jnp.int32, (d, d), 0) == lax.broadcasted_iota(jnp.int32, (d, d), 1)).astype(f32)
    ones8 = jnp.ones((8, d), bf16)
    onesd = jnp.ones((d, d), bf16)

    group = 4
    for first in range(0, heads, group):
        hs = list(range(first, first + group))
        ks, lower, ncol, nrow, invs = {}, {}, {}, {}, {}
        for h in hs:
            k = k_ref[:, h * d : (h + 1) * d]
            kf = k.astype(f32)
            sq = split2(kf * kf)
            n_c = lax.rsqrt(sum(mm(p, onesd) for p in sq) + eps_norm)
            n_r = lax.rsqrt(sum(nt(ones8, p) for p in sq) + eps_norm)[:1]
            gram = nt(k, k)
            gap = jnp.where(strict, c_col[:, h : h + 1] - c_row[h : h + 1, :], 0.0)
            n_cc = jnp.concatenate([n_c] * (steps // d), axis=1)
            low = jnp.where(strict, jnp.exp(gap) * gram * (2.0 * n_r) * n_cc, 0.0)
            ks[h], lower[h], ncol[h], nrow[h] = k, low, n_c, n_r
            diag = [low[:half, :half], low[half:, half:]]
            m = (hi_ // 2 == hj_ // 2)
            invs[h] = [eye - jnp.where(m, x, 0.0) for x in diag]
        b = 2
        while b < half:
            m = (hi_ // (2 * b) == hj_ // (2 * b)) & ((hi_ // b) % 2 == 1) & ((hj_ // b) % 2 == 0)
            for h in hs:
                for s in range(2):
                    block = lower[h][s * half : (s + 1) * half, s * half : (s + 1) * half]
                    off = jnp.where(m, block, 0.0)
                    iw = split2(invs[h][s])
                    iww = jnp.concatenate(iw, axis=1)
                    t = mm4(iww, square(off), half)
                    invs[h][s] = invs[h][s] - mm4(wide(t), jnp.concatenate([iww, iww], axis=0), half)
            b *= 2
        for h in hs:
            t = mm4(wide(invs[h][1]), square(lower[h][half:, :half]), half)
            c21 = -mm4(wide(t), square(invs[h][0]), half)
            minv = jnp.concatenate(
                [
                    jnp.concatenate([invs[h][0], jnp.zeros((half, half), f32)], axis=1),
                    jnp.concatenate([c21, invs[h][1]], axis=1),
                ],
                axis=0,
            )
            k = ks[h]
            v = v_ref[:, h * d : (h + 1) * d]
            y = sum(mm(p, v) for p in split2(minv))
            grow = jnp.exp(c_row[h : h + 1, :]) * nrow[h]
            w = sum(mm(p, k) for p in split2(minv * grow))
            last = c_col[steps - 1 :, h : h + 1]
            tail = jnp.exp(last - c_col[:, h : h + 1]) * ncol[h]
            kt = jnp.transpose(k.astype(f32)).astype(bf16)
            yw = jnp.concatenate([tail * y, tail * w], axis=1)
            ba = sum(mm(kt, p) for p in split2(2.0 * yw))
            b_ref[h] = ba[:, :d]
            aw_ref[h] = wide(jnp.exp(last) * eye_d - ba[:, d:])
            q = q_ref[:, h * d : (h + 1) * d]
            qc = q_col[:, h : h + 1]
            qgap = jnp.where(visible, qc - c_row[h : h + 1, :], 0.0)
            pairs = jnp.where(visible, jnp.exp(qgap) * nt(q, k) * (2.0 * nrow[h]), 0.0)
            p_hi, p_lo = split2(pairs)
            x_hi, x_lo = split2(jnp.concatenate([y, w], axis=1))
            px = mm(p_hi, x_hi) + mm(p_lo, x_hi) + mm(p_hi, x_lo)
            lo_ref[h] = px[:, :d]
            r_ref[h] = wide(jnp.exp(qc) * q.astype(f32) - px[:, d:])


def chain_kernel(inner, count, aw_ref, b_ref, r_ref, lo_ref, gate_ref, gain_ref, o_ref,
                 s_in, s_out, send_sem, recv_sem):
    heads, d = b_ref.shape[0], b_ref.shape[1]
    me = lax.axis_index("outer") * inner + lax.axis_index("inner")

    def place(i):
        return {"outer": i // inner, "inner": i % inner}

    barrier = pltpu.get_barrier_semaphore()

    @pl.when(me > 0)
    def _():
        pl.semaphore_signal(barrier, inc=1, device_id=place(me - 1), device_id_type=MESH)

    @pl.when(me < count - 1)
    def _():
        pl.semaphore_wait(barrier, 1)

    def copy(h):
        return pltpu.make_async_remote_copy(
            src_ref=s_out.at[h], dst_ref=s_in.at[h],
            send_sem=send_sem.at[h], recv_sem=recv_sem.at[h],
            device_id=place(me + 1), device_id_type=MESH,
        )

    @pl.when(me == 0)
    def _():
        for h in range(heads):
            s_in[h] = jnp.zeros((d, d), f32)

    for h in range(heads):
        @pl.when(me > 0)
        def _():
            copy(h).wait_recv()

        @pl.when(me < count - 1)
        def _():
            s_out[h] = mm4(aw_ref[h], square(s_in[h]), d) + b_ref[h]
            copy(h).start()

    gain = gain_ref[...]
    for h in range(heads):
        out = mm4(r_ref[h], square(s_in[h]), d) + lo_ref[h]
        scale = lax.rsqrt(jnp.mean(out * out, axis=-1, keepdims=True) + eps_norm)
        g = gate_ref[:, h * d : (h + 1) * d].astype(f32)
        o_ref[:, h * d : (h + 1) * d] = (out * scale * gain * (g / (1.0 + jnp.exp(-g)))).astype(bf16)

    @pl.when(me < count - 1)
    def _():
        for h in range(heads):
            copy(h).wait_send()


def vmem_specs(n):
    return [pl.BlockSpec(memory_space=pltpu.VMEM)] * n


def solution(mesh):
    inner = mesh.shape["inner"]
    count = inner * mesh.shape["outer"]

    def local(queries, keys, values, log_gate, out_gate, norm_gain):
        toks, width = queries.shape
        heads = log_gate.shape[1]
        d = width // heads
        steps = 2 * toks
        mats = jax.ShapeDtypeStruct((heads, d, d), f32)
        wides = jax.ShapeDtypeStruct((heads, d, 2 * d), bf16)
        aw, b, r, lo = pl.pallas_call(
            local_kernel,
            out_shape=(wides, mats, wides, mats),
            in_specs=vmem_specs(4),
            out_specs=tuple(vmem_specs(4)),
            compiler_params=pltpu.CompilerParams(vmem_limit_bytes=48 << 20),
            name="local_maps",
        )(keys.reshape(steps, width), values.reshape(steps, width), queries, log_gate.T)
        return pl.pallas_call(
            lambda *refs: chain_kernel(inner, count, *refs),
            out_shape=jax.ShapeDtypeStruct((toks, width), bf16),
            in_specs=vmem_specs(6),
            out_specs=vmem_specs(1)[0],
            scratch_shapes=[
                pltpu.VMEM((heads, d, d), f32),
                pltpu.VMEM((heads, d, d), f32),
                pltpu.SemaphoreType.DMA((heads,)),
                pltpu.SemaphoreType.DMA((heads,)),
            ],
            compiler_params=pltpu.CompilerParams(collective_id=0, has_side_effects=True),
            name="chain",
        )(aw, b, r, lo, out_gate, norm_gain.reshape(1, d))

    spec = P(("groups", "outer", "inner"), None)
    spec3 = P(("groups", "outer", "inner"), None, None)
    return jax.shard_map(
        local, mesh=mesh, in_specs=(spec, spec3, spec3, spec, spec, P()), out_specs=spec, check_vma=False
    )
```

```python
import jax
import jax.numpy as jnp
from jax import lax
from jax.experimental import pallas as pl
from jax.experimental.pallas import tpu as pltpu
from jax.sharding import PartitionSpec as P

eps_norm = 1e-06
f32 = jnp.float32
bf16 = jnp.bfloat16
MESH = pl.DeviceIdType.MESH
NT = (((1,), (1,)), ((), ()))
TN = (((0,), (0,)), ((), ()))


def mm(a, b):
    return jnp.dot(a, b, preferred_element_type=f32)


def split2(x):
    hi = x.astype(bf16)
    return hi, (x - hi.astype(f32)).astype(bf16)


def split3(x):
    hi, rest = x.astype(bf16), None
    rest = x - hi.astype(f32)
    mid = rest.astype(bf16)
    return hi, mid, (rest - mid.astype(f32)).astype(bf16)


def wide(x):
    return jnp.concatenate(split2(x), axis=1)


def square(x):
    row = jnp.concatenate(split2(x), axis=1)
    return jnp.concatenate([row, row], axis=0)


def mm4(a_wide, b_square, size):
    both = mm(a_wide, b_square)
    return both[:, :size] + both[:, size:]


def square_t(x):
    hi, lo = split2(x)
    return jnp.concatenate(
        [jnp.concatenate([hi, hi], axis=1), jnp.concatenate([lo, lo], axis=1)], axis=0
    )


def iotas(r, c):
    return (
        lax.broadcasted_iota(jnp.int32, (r, c), 0),
        lax.broadcasted_iota(jnp.int32, (r, c), 1),
    )


def nt(a, b):
    return lax.dot_general(a, b, NT, preferred_element_type=f32)


def kernel(inner, count, k_ref, v_ref, q_ref, lg_ref, gate_ref, gain_ref, o_ref,
           maps, whole_sq, whole_b, first_sq, r_ref, lo_ref, s_in, s_out, states,
           pair_send, pair_recv, chain_send, chain_recv, state_send, state_recv):
    steps = k_ref.shape[0]
    toks = q_ref.shape[0]
    heads = lg_ref.shape[0]
    d = k_ref.shape[1] // heads
    half = steps // 2
    kept = heads // 2
    parts = chain_send.shape[1]
    rows = d // parts

    me = lax.axis_index("outer") * inner + lax.axis_index("inner")
    par = me % 2
    mate = me + 1 - 2 * par
    has_next = me < count - 2

    def place(i):
        return {"outer": i // inner, "inner": i % inner}

    barrier = pltpu.get_barrier_semaphore()
    pl.semaphore_signal(barrier, inc=1, device_id=place(mate), device_id_type=MESH)

    @pl.when(me >= 2)
    def _():
        pl.semaphore_signal(barrier, inc=1, device_id=place(me - 2), device_id_type=MESH)

    def remote(src, dst, send, recv, target):
        return pltpu.make_async_remote_copy(
            src_ref=src, dst_ref=dst, send_sem=send, recv_sem=recv,
            device_id=place(target), device_id_type=MESH,
        )

    def pair_copy(i):
        h = i + kept * par
        return remote(maps.at[par, h], maps.at[par, h], pair_send.at[i], pair_recv.at[i], mate)

    def chain_copy(i, c):
        piece = pl.ds(c * rows, rows)
        return remote(s_out.at[i, piece], s_in.at[0, i, piece],
                      chain_send.at[i, c], chain_recv.at[i, c], me + 2)

    def state_copy(i):
        return remote(s_in.at[1 - par, i], states.at[i], state_send.at[i], state_recv.at[i], mate)

    i_st, j_tk = iotas(steps, toks)
    tri_steps = (j_tk <= i_st // 2).astype(f32).astype(bf16)
    i_tk, j_tk2 = iotas(toks, toks)
    tri_toks = (j_tk2 <= i_tk).astype(f32).astype(bf16)
    lgs = split3(lg_ref[...])
    c_col = sum(nt(tri_steps, p) for p in lgs)
    q_col = sum(nt(tri_toks, p) for p in lgs)
    c_row = sum(nt(p, tri_steps) for p in lgs)
    ii, jj = iotas(steps, steps)
    strict = ii > jj
    it, jt = iotas(toks, steps)
    visible = jt <= 2 * it + 1
    hi_, hj_ = iotas(half, half)
    eye = (hi_ == hj_).astype(f32)
    di, dj = iotas(d, d)
    eye_d = (di == dj).astype(f32)
    ones8 = jnp.ones((8, d), bf16)
    onesd = jnp.ones((d, d), bf16)

    ks, nrow, solved = {}, {}, {}
    quarter = kept // 2
    for turn in range(2):
        hs = [turn * quarter + x for x in range(quarter)]
        hs = hs + [kept + x for x in hs]
        lower, ncol, invs = {}, {}, {}
        for h in hs:
            k = k_ref[:, h * d : (h + 1) * d]
            kf = k.astype(f32)
            sq = split2(kf * kf)
            n_c = lax.rsqrt(sum(mm(p, onesd) for p in sq) + eps_norm)
            n_r = lax.rsqrt(sum(nt(ones8, p) for p in sq) + eps_norm)[:1]
            gram = nt(k, k)
            gap = jnp.where(strict, c_col[:, h : h + 1] - c_row[h : h + 1, :], 0.0)
            n_cc = jnp.concatenate([n_c] * (steps // d), axis=1)
            low = jnp.where(strict, jnp.exp(gap) * gram * (2.0 * n_r) * n_cc, 0.0)
            ks[h], lower[h], ncol[h], nrow[h] = k, low, n_c, n_r
            diag = [low[:half, :half], low[half:, half:]]
            m = hi_ // 2 == hj_ // 2
            invs[h] = [eye - jnp.where(m, x, 0.0) for x in diag]
        b = 2
        while b < half:
            m = (hi_ // (2 * b) == hj_ // (2 * b)) & ((hi_ // b) % 2 == 1) & ((hj_ // b) % 2 == 0)
            for h in hs:
                for s in range(2):
                    block = lower[h][s * half : (s + 1) * half, s * half : (s + 1) * half]
                    off = jnp.where(m, block, 0.0)
                    iww = wide(invs[h][s])
                    t = mm4(iww, square(off), half)
                    invs[h][s] = invs[h][s] - mm4(wide(t), jnp.concatenate([iww, iww], axis=0), half)
            b *= 2
        for h in hs:
            t = mm4(wide(invs[h][1]), square(lower[h][half:, :half]), half)
            c21 = -mm4(wide(t), square(invs[h][0]), half)
            minv = jnp.concatenate(
                [
                    jnp.concatenate([invs[h][0], jnp.zeros((half, half), f32)], axis=1),
                    jnp.concatenate([c21, invs[h][1]], axis=1),
                ],
                axis=0,
            )
            k = ks[h]
            v = v_ref[:, h * d : (h + 1) * d]
            y = sum(mm(p, v) for p in split2(minv))
            grow = jnp.exp(c_row[h : h + 1, :]) * nrow[h]
            w = sum(mm(p, k) for p in split2(minv * grow))
            last = c_col[steps - 1 :, h : h + 1]
            tail = jnp.exp(last - c_col[:, h : h + 1]) * (2.0 * ncol[h])
            kt = jnp.transpose(k.astype(f32)).astype(bf16)
            wy = jnp.concatenate([tail * w, tail * y], axis=1)
            ab = jnp.transpose(sum(mm(kt, p) for p in split2(wy)))
            maps[par, h] = jnp.concatenate([jnp.exp(last) * eye_d - ab[:d], ab[d:]], axis=0)
            solved[h] = (y, w)
        if turn == 0:
            @pl.when(has_next)
            def _():
                pl.semaphore_wait(barrier, 2)

            @pl.when(me >= count - 2)
            def _():
                pl.semaphore_wait(barrier, 1)
        for i in range(turn * quarter, (turn + 1) * quarter):
            pair_copy(i).start()

    for h in range(heads):
        k = ks[h]
        y, w = solved[h]
        q = q_ref[:, h * d : (h + 1) * d]
        qc = q_col[:, h : h + 1]
        qgap = jnp.where(visible, qc - c_row[h : h + 1, :], 0.0)
        pairs = jnp.where(visible, jnp.exp(qgap) * nt(q, k) * (2.0 * nrow[h]), 0.0)
        p_hi, p_lo = split2(pairs)
        x_hi, x_lo = split2(jnp.concatenate([y, w], axis=1))
        px = mm(p_hi, x_hi) + mm(p_lo, x_hi) + mm(p_hi, x_lo)
        lo_ref[h] = px[:, :d]
        r_ref[h] = wide(jnp.exp(qc) * q.astype(f32) - px[:, d:])

    @pl.when(me < 2)
    def _():
        for i in range(kept):
            s_in[0, i] = jnp.zeros((d, d), f32)

    mine = kept * (1 - par)
    for i in range(kept):
        pair_copy(i).wait_recv()
        at_later = square(maps[1, mine + i, :d])
        both = mm4(wide(maps[0, mine + i]), at_later, d)
        whole_sq[i] = square(both[:d])
        whole_b[i] = both[d:] + maps[1, mine + i, d:]
        first_sq[i] = square(maps[0, mine + i, :d])

    for i in range(kept):
        for c in range(parts):
            lo, hi = c * rows, (c + 1) * rows

            @pl.when((me >= 2) & has_next)
            def _():
                chain_copy(i, c).wait_recv()

            @pl.when(has_next)
            def _():
                s_out[i, lo:hi] = mm4(wide(s_in[0, i, lo:hi]), whole_sq[i], d) + whole_b[i, lo:hi]
                chain_copy(i, c).start()

    gain = gain_ref[...]

    def readout(h, state_t):
        both = nt(r_ref[h], square_t(state_t))
        out = both[:, :d] + both[:, d:] + lo_ref[h]
        scale = lax.rsqrt(jnp.mean(out * out, axis=-1, keepdims=True) + eps_norm)
        cols = pl.ds(pl.multiple_of(h * d, d), d)
        g = gate_ref[:, cols].astype(f32)
        o_ref[:, cols] = (out * scale * gain * (g / (1.0 + jnp.exp(-g)))).astype(bf16)

    for i in range(kept):
        @pl.when((me >= 2) & (me >= count - 2))
        def _():
            for c in range(parts):
                chain_copy(i, c).wait_recv()

        s_in[1, i] = mm4(wide(s_in[0, i]), first_sq[i], d) + maps[0, mine + i, d:]
        state_copy(i).start()
    for i in range(kept):
        readout(mine + i, s_in[par, i])
    for i in range(kept):
        state_copy(i).wait_recv()
        readout(kept * par + i, states[i])

    for i in range(kept):
        pair_copy(i).wait_send()
        state_copy(i).wait_send()

    @pl.when(has_next)
    def _():
        for i in range(kept):
            for c in range(parts):
                chain_copy(i, c).wait_send()


def vmem_specs(n):
    return [pl.BlockSpec(memory_space=pltpu.VMEM)] * n


def solution(mesh):
    inner = mesh.shape["inner"]
    count = inner * mesh.shape["outer"]
    assert inner % 2 == 0

    def local(queries, keys, values, log_gate, out_gate, norm_gain):
        toks, width = queries.shape
        heads = log_gate.shape[1]
        d = width // heads
        steps = 2 * toks
        kept = heads // 2
        parts = 2
        dma = pltpu.SemaphoreType.DMA
        return pl.pallas_call(
            lambda *refs: kernel(inner, count, *refs),
            out_shape=jax.ShapeDtypeStruct((toks, width), bf16),
            in_specs=vmem_specs(6),
            out_specs=vmem_specs(1)[0],
            scratch_shapes=[
                pltpu.VMEM((2, heads, 2 * d, d), f32),
                pltpu.VMEM((kept, 2 * d, 2 * d), bf16),
                pltpu.VMEM((kept, d, d), f32),
                pltpu.VMEM((kept, 2 * d, 2 * d), bf16),
                pltpu.VMEM((heads, d, 2 * d), bf16),
                pltpu.VMEM((heads, d, d), f32),
                pltpu.VMEM((2, kept, d, d), f32),
                pltpu.VMEM((kept, d, d), f32),
                pltpu.VMEM((kept, d, d), f32),
                dma((kept,)), dma((kept,)), dma((kept, parts)), dma((kept, parts)), dma((kept,)), dma((kept,)),
            ],
            compiler_params=pltpu.CompilerParams(
                collective_id=0, has_side_effects=True, vmem_limit_bytes=48 << 20
            ),
            name="delta_product",
        )(keys.reshape(steps, width), values.reshape(steps, width), queries, log_gate.T,
          out_gate, norm_gain.reshape(1, d))

    spec = P(("groups", "outer", "inner"), None)
    spec3 = P(("groups", "outer", "inner"), None, None)
    return jax.shard_map(
        local, mesh=mesh, in_specs=(spec, spec3, spec3, spec, spec, P()), out_specs=spec, check_vma=False
    )
```

```python
import jax
import jax.numpy as jnp
from jax import lax
from jax.experimental import pallas as pl
from jax.experimental.pallas import tpu as pltpu
from jax.sharding import PartitionSpec as P

eps_norm = 1e-06
f32 = jnp.float32
bf16 = jnp.bfloat16
MESH = pl.DeviceIdType.MESH
NT = (((1,), (1,)), ((), ()))
TN = (((0,), (0,)), ((), ()))


def mm(a, b):
    return jnp.dot(a, b, preferred_element_type=f32)


def split2(x):
    hi = x.astype(bf16)
    return hi, (x - hi.astype(f32)).astype(bf16)


def split3(x):
    hi, rest = x.astype(bf16), None
    rest = x - hi.astype(f32)
    mid = rest.astype(bf16)
    return hi, mid, (rest - mid.astype(f32)).astype(bf16)


def wide(x):
    return jnp.concatenate(split2(x), axis=1)


def square(x):
    row = jnp.concatenate(split2(x), axis=1)
    return jnp.concatenate([row, row], axis=0)


def mm4(a_wide, b_square, size):
    both = mm(a_wide, b_square)
    return both[:, :size] + both[:, size:]


def square_t(x):
    hi, lo = split2(x)
    return jnp.concatenate(
        [jnp.concatenate([hi, hi], axis=1), jnp.concatenate([lo, lo], axis=1)], axis=0
    )


def iotas(r, c):
    return (
        lax.broadcasted_iota(jnp.int32, (r, c), 0),
        lax.broadcasted_iota(jnp.int32, (r, c), 1),
    )


def nt(a, b):
    return lax.dot_general(a, b, NT, preferred_element_type=f32)


def kernel(inner, count, k_ref, v_ref, q_ref, lg_ref, gate_ref, gain_ref, o_ref,
           maps, whole_sq, whole_b, first_sq, r_ref, lo_ref, s_in, s_out, states,
           pair_send, pair_recv, chain_send, chain_recv, state_send, state_recv):
    steps = k_ref.shape[0]
    toks = q_ref.shape[0]
    heads = lg_ref.shape[0]
    d = k_ref.shape[1] // heads
    half = steps // 2
    kept = heads // 2
    parts = chain_send.shape[1]
    rows = d // parts

    me = lax.axis_index("outer") * inner + lax.axis_index("inner")
    par = me % 2
    mate = me + 1 - 2 * par
    has_next = me < count - 2
    early = me < inner

    def place(i):
        return {"outer": i // inner, "inner": i % inner}

    barrier = pltpu.get_barrier_semaphore()
    pl.semaphore_signal(barrier, inc=1, device_id=place(mate), device_id_type=MESH)

    @pl.when(me >= 2)
    def _():
        pl.semaphore_signal(barrier, inc=1, device_id=place(me - 2), device_id_type=MESH)

    def remote(src, dst, send, recv, target):
        return pltpu.make_async_remote_copy(
            src_ref=src, dst_ref=dst, send_sem=send, recv_sem=recv,
            device_id=place(target), device_id_type=MESH,
        )

    def pair_copy(i):
        h = i + kept * par
        return remote(maps.at[par, h], maps.at[par, h], pair_send.at[i], pair_recv.at[i], mate)

    def chain_copy(i, c):
        piece = pl.ds(c * rows, rows)
        return remote(s_out.at[i, piece], s_in.at[0, i, piece],
                      chain_send.at[i, c], chain_recv.at[i, c], me + 2)

    def state_copy(i):
        return remote(s_in.at[1 - par, i], states.at[i], state_send.at[i], state_recv.at[i], mate)

    i_st, j_tk = iotas(steps, toks)
    tri_steps = (j_tk <= i_st // 2).astype(f32).astype(bf16)
    i_tk, j_tk2 = iotas(toks, toks)
    tri_toks = (j_tk2 <= i_tk).astype(f32).astype(bf16)
    lgs = split3(lg_ref[...])
    c_col = sum(nt(tri_steps, p) for p in lgs)
    q_col = sum(nt(tri_toks, p) for p in lgs)
    c_row = sum(nt(p, tri_steps) for p in lgs)
    ii, jj = iotas(steps, steps)
    strict = ii > jj
    it, jt = iotas(toks, steps)
    visible = jt <= 2 * it + 1
    hi_, hj_ = iotas(half, half)
    eye = (hi_ == hj_).astype(f32)
    di, dj = iotas(d, d)
    eye_d = (di == dj).astype(f32)
    ones8 = jnp.ones((8, d), bf16)
    onesd = jnp.ones((d, d), bf16)

    ks, nrow, solved = {}, {}, {}
    quarter = kept // 2
    for turn in range(2):
        hs = [turn * quarter + x for x in range(quarter)]
        hs = hs + [kept + x for x in hs]
        lower, ncol, invs = {}, {}, {}
        for h in hs:
            k = k_ref[:, h * d : (h + 1) * d]
            kf = k.astype(f32)
            sq = split2(kf * kf)
            n_c = lax.rsqrt(sum(mm(p, onesd) for p in sq) + eps_norm)
            n_r = lax.rsqrt(sum(nt(ones8, p) for p in sq) + eps_norm)[:1]
            gram = nt(k, k)
            gap = jnp.where(strict, c_col[:, h : h + 1] - c_row[h : h + 1, :], 0.0)
            n_cc = jnp.concatenate([n_c] * (steps // d), axis=1)
            low = jnp.where(strict, jnp.exp(gap) * gram * (2.0 * n_r) * n_cc, 0.0)
            ks[h], lower[h], ncol[h], nrow[h] = k, low, n_c, n_r
            diag = [low[:half, :half], low[half:, half:]]
            m = hi_ // 2 == hj_ // 2
            invs[h] = [eye - jnp.where(m, x, 0.0) for x in diag]
        b = 2
        while b < half:
            m = (hi_ // (2 * b) == hj_ // (2 * b)) & ((hi_ // b) % 2 == 1) & ((hj_ // b) % 2 == 0)
            for h in hs:
                for s in range(2):
                    block = lower[h][s * half : (s + 1) * half, s * half : (s + 1) * half]
                    off = jnp.where(m, block, 0.0)
                    iww = wide(invs[h][s])
                    t = mm4(iww, square(off), half)
                    invs[h][s] = invs[h][s] - mm4(wide(t), jnp.concatenate([iww, iww], axis=0), half)
            b *= 2
        for h in hs:
            t = mm4(wide(invs[h][1]), square(lower[h][half:, :half]), half)
            c21 = -mm4(wide(t), square(invs[h][0]), half)
            minv = jnp.concatenate(
                [
                    jnp.concatenate([invs[h][0], jnp.zeros((half, half), f32)], axis=1),
                    jnp.concatenate([c21, invs[h][1]], axis=1),
                ],
                axis=0,
            )
            k = ks[h]
            v = v_ref[:, h * d : (h + 1) * d]
            y = sum(mm(p, v) for p in split2(minv))
            grow = jnp.exp(c_row[h : h + 1, :]) * nrow[h]
            w = sum(mm(p, k) for p in split2(minv * grow))
            last = c_col[steps - 1 :, h : h + 1]
            tail = jnp.exp(last - c_col[:, h : h + 1]) * (2.0 * ncol[h])
            kt = jnp.transpose(k.astype(f32)).astype(bf16)
            wy = jnp.concatenate([tail * w, tail * y], axis=1)
            ab = jnp.transpose(sum(mm(kt, p) for p in split2(wy)))
            maps[par, h] = jnp.concatenate([jnp.exp(last) * eye_d - ab[:d], ab[d:]], axis=0)
            solved[h] = (y, w)
        if turn == 0:
            @pl.when(has_next)
            def _():
                pl.semaphore_wait(barrier, 2)

            @pl.when(me >= count - 2)
            def _():
                pl.semaphore_wait(barrier, 1)

        @pl.when(early)
        def _():
            for i in range(turn * quarter, (turn + 1) * quarter):
                pair_copy(i).start()

    mine = kept * (1 - par)

    def merge(i):
        pair_copy(i).wait_recv()
        at_later = square(maps[1, mine + i, :d])
        both = mm4(wide(maps[0, mine + i]), at_later, d)
        whole_sq[i] = square(both[:d])
        whole_b[i] = both[d:] + maps[1, mine + i, d:]
        first_sq[i] = square(maps[0, mine + i, :d])

    @pl.when(me < 2)
    def _():
        for i in range(kept):
            s_in[0, i] = jnp.zeros((d, d), f32)

    def forward(i, c):
        lo, hi = c * rows, (c + 1) * rows
        s_out[i, lo:hi] = mm4(wide(s_in[0, i, lo:hi]), whole_sq[i], d) + whole_b[i, lo:hi]
        chain_copy(i, c).start()

    @pl.when(early)
    def _():
        for i in range(quarter):
            merge(i)

            @pl.when((me < 2) & has_next)
            def _():
                for c in range(parts):
                    forward(i, c)

    for h in range(heads):
        k = ks[h]
        y, w = solved[h]
        q = q_ref[:, h * d : (h + 1) * d]
        qc = q_col[:, h : h + 1]
        qgap = jnp.where(visible, qc - c_row[h : h + 1, :], 0.0)
        pairs = jnp.where(visible, jnp.exp(qgap) * nt(q, k) * (2.0 * nrow[h]), 0.0)
        p_hi, p_lo = split2(pairs)
        x_hi, x_lo = split2(jnp.concatenate([y, w], axis=1))
        px = mm(p_hi, x_hi) + mm(p_lo, x_hi) + mm(p_hi, x_lo)
        lo_ref[h] = px[:, :d]
        r_ref[h] = wide(jnp.exp(qc) * q.astype(f32) - px[:, d:])

    @pl.when(jnp.logical_not(early))
    def _():
        for i in range(kept):
            pair_copy(i).start()
        for i in range(quarter):
            merge(i)

    for i in range(quarter, kept):
        merge(i)

        @pl.when((me < 2) & has_next)
        def _():
            for c in range(parts):
                forward(i, c)

    @pl.when((me >= 2) & has_next)
    def _():
        for i in range(kept):
            for c in range(parts):
                chain_copy(i, c).wait_recv()
                forward(i, c)

    gain = gain_ref[...]

    def readout(h, state_t):
        both = nt(r_ref[h], square_t(state_t))
        out = both[:, :d] + both[:, d:] + lo_ref[h]
        scale = lax.rsqrt(jnp.mean(out * out, axis=-1, keepdims=True) + eps_norm)
        cols = pl.ds(pl.multiple_of(h * d, d), d)
        g = gate_ref[:, cols].astype(f32)
        o_ref[:, cols] = (out * scale * gain * (g / (1.0 + jnp.exp(-g)))).astype(bf16)

    for i in range(kept):
        @pl.when((me >= 2) & (me >= count - 2))
        def _():
            for c in range(parts):
                chain_copy(i, c).wait_recv()

        s_in[1, i] = mm4(wide(s_in[0, i]), first_sq[i], d) + maps[0, mine + i, d:]
        state_copy(i).start()
        readout(mine + i, s_in[par, i])
    for i in range(kept):
        state_copy(i).wait_recv()
        readout(kept * par + i, states[i])

    for i in range(kept):
        pair_copy(i).wait_send()
        state_copy(i).wait_send()

    @pl.when(has_next)
    def _():
        for i in range(kept):
            for c in range(parts):
                chain_copy(i, c).wait_send()


def vmem_specs(n):
    return [pl.BlockSpec(memory_space=pltpu.VMEM)] * n


def solution(mesh):
    inner = mesh.shape["inner"]
    count = inner * mesh.shape["outer"]
    assert inner % 2 == 0

    def local(queries, keys, values, log_gate, out_gate, norm_gain):
        toks, width = queries.shape
        heads = log_gate.shape[1]
        d = width // heads
        steps = 2 * toks
        kept = heads // 2
        parts = 2
        dma = pltpu.SemaphoreType.DMA
        return pl.pallas_call(
            lambda *refs: kernel(inner, count, *refs),
            out_shape=jax.ShapeDtypeStruct((toks, width), bf16),
            in_specs=vmem_specs(6),
            out_specs=vmem_specs(1)[0],
            scratch_shapes=[
                pltpu.VMEM((2, heads, 2 * d, d), f32),
                pltpu.VMEM((kept, 2 * d, 2 * d), bf16),
                pltpu.VMEM((kept, d, d), f32),
                pltpu.VMEM((kept, 2 * d, 2 * d), bf16),
                pltpu.VMEM((heads, d, 2 * d), bf16),
                pltpu.VMEM((heads, d, d), f32),
                pltpu.VMEM((2, kept, d, d), f32),
                pltpu.VMEM((kept, d, d), f32),
                pltpu.VMEM((kept, d, d), f32),
                dma((kept,)), dma((kept,)), dma((kept, parts)), dma((kept, parts)), dma((kept,)), dma((kept,)),
            ],
            compiler_params=pltpu.CompilerParams(
                collective_id=0, has_side_effects=True, vmem_limit_bytes=48 << 20
            ),
            name="delta_product",
        )(keys.reshape(steps, width), values.reshape(steps, width), queries, log_gate.T,
          out_gate, norm_gain.reshape(1, d))

    spec = P(("groups", "outer", "inner"), None)
    spec3 = P(("groups", "outer", "inner"), None, None)
    return jax.shard_map(
        local, mesh=mesh, in_specs=(spec, spec3, spec3, spec, spec, P()), out_specs=spec, check_vma=False
    )
```
